256 devices in a mesh: dp: 2 (over core), ctx: 32 (over z, y), head: 4 (over x).
Axes of the slice: x: 4, y: 4, z: 8, core: 2. Of those that a mesh axis runs over, the one named last changes fastest.
Arguments:
- queries: bfloat16 [16384, 1536], P(('dp', 'ctx'), 'head'), parts along dimension 0, may hold values from -5 to 5
- keys: bfloat16 [16384, 1536], P(('dp', 'ctx'), 'head'), parts along dimension 0, may hold values from -5 to 5
- values: bfloat16 [16384, 1536], P(('dp', 'ctx'), 'head'), parts along dimension 0, may hold values from -6 to 6
- out_grad: bfloat16 [16384, 1536], P(('dp', 'ctx'), 'head'), parts along dimension 0, may hold values from -6 to 6
- radial_pick: int32 [32, 32], replicated, may hold values from 0 to 15
Outputs:
- attended: bfloat16 [16384, 1536], P(('dp', 'ctx'), 'head'), parts along dimension 0
- query_grad: bfloat16 [16384, 1536], P(('dp', 'ctx'), 'head'), parts along dimension 0
- key_grad: bfloat16 [16384, 1536], P(('dp', 'ctx'), 'head'), parts along dimension 0
- value_grad: bfloat16 [16384, 1536], P(('dp', 'ctx'), 'head'), parts along dimension 0
The draws below stay inside these ranges and needn't reach their ends.
There are 2 independent parts, one for each index of `dp`. The reference program is written for one: setup_inputs(seed, part) draws one part's arguments, and reference() takes and returns one part's arrays. A program takes and returns all parts, laid end to end along the dimension named above; an argument that names none is the same for every part. Nothing has to cross between parts.
All inputs are finite; a program needn't handle non-finite values.
Results may differ from the reference program's by a relative error of at most 0.02.
Values may be sent and summed in bfloat16 or wider, within the bound.
A program may use at most 128 MiB of HBM per device.

```python
import jax
import jax.numpy as jnp
from jax import lax

HEADS = 12
HD = 128
BLOCK = 64
FT = 256
NF = 32
TOKENS = 8192


def draw_queries(key, part):
    values = jnp.clip(jax.random.normal(jax.random.fold_in(key, 1), (TOKENS, HEADS * HD), jnp.float32), -4.5, 4.5)
    return values.astype(jnp.bfloat16)


def draw_keys(key, part):
    values = jnp.clip(jax.random.normal(jax.random.fold_in(key, 2), (TOKENS, HEADS * HD), jnp.float32), -4.5, 4.5)
    return values.astype(jnp.bfloat16)


def with_ends(entries, stream_key, smallest, largest):
    longest = entries.shape.index(max(entries.shape))
    spots = []
    for shift in (0, 1):
        where = [jax.random.randint(jax.random.fold_in(stream_key, axis), (), 0, length) for axis, length in enumerate(entries.shape)]
        where[longest] = (where[longest] + shift) % entries.shape[longest]
        spots.append(tuple(where))
    return entries.at[spots[0]].set(smallest).at[spots[1]].set(largest)


def block_levels(own_key, extent, cuts, smallest, top_value):
    gain = 1.0
    for position, blocks in cuts:
        heights = jax.random.uniform(jax.random.fold_in(jax.random.fold_in(own_key, 6), position), (blocks,), jnp.float32, smallest / len(cuts), top_value / len(cuts))
        gain = gain * jnp.repeat(jnp.exp(heights), extent[position] // blocks).reshape((-1,) + (1,) * (len(extent) - 1 - position))
    return gain


def scatter_about(key, dims, scale, reach, shards=(), kind=jnp.bfloat16):
    entries = jax.random.normal(key, dims, jnp.float32) * scale
    if len(shards) > 0:
        entries = block_levels(key, dims, shards, -0.22, 0.18) * entries
    return jnp.clip(entries, min=-reach, max=reach).astype(kind)


def setup_inputs(seed: int = 0, part: int = 0) -> dict:
    streams_of = jax.random.split(jax.random.key(seed), 6)
    part_keys = jax.random.split(jax.random.fold_in(streams_of[5], part), 6)
    return {
        "queries": draw_queries(jax.random.fold_in(jax.random.fold_in(streams_of[5], part), 71), part),
        "keys": draw_keys(jax.random.fold_in(jax.random.fold_in(streams_of[5], part), 71), part),
        "values": scatter_about(part_keys[2], (TOKENS, HEADS * HD), 1.0, 6.0, ((0, 32), (1, 4))),
        "out_grad": scatter_about(part_keys[3], (TOKENS, HEADS * HD), 1.0, 6.0, ((0, 32), (1, 4))),
        "radial_pick": with_ends(jax.random.randint(streams_of[4], (NF, NF), 0, (FT // BLOCK) * (FT // BLOCK)), jax.random.fold_in(streams_of[4], 1), 0, ((FT // BLOCK) * (FT // BLOCK)) - 1).astype(jnp.int32),
    }


def frame_mask(frame, pick_row, frames):
    blocks = FT // BLOCK
    tile = jnp.arange(FT, dtype=jnp.int32) // BLOCK
    near_frame = frame - 1 + jnp.arange(3 * FT, dtype=jnp.int32) // FT
    near_live = (near_frame >= 0) & (near_frame < frames)
    near_mask = jnp.broadcast_to(near_live[None, :], (FT, 3 * FT))
    slot = jnp.arange(frames * BLOCK, dtype=jnp.int32) // BLOCK
    distance = jnp.abs(frame - slot)
    chosen = jnp.repeat(pick_row, BLOCK) // blocks
    far_mask = (distance[None, :] >= 2) & ((distance[None, :] < 4) | (tile[:, None] == chosen[None, :]))
    return jnp.concatenate([near_mask, far_mask], axis=1)


def reference(queries, keys, values, out_grad, radial_pick):
    frames = TOKENS // FT
    blocks = FT // BLOCK
    width = HEADS * HD
    scale = HD ** -0.5
    zero_frame = jnp.zeros((1, FT, width), keys.dtype)
    key_padded = jnp.concatenate([zero_frame, keys.reshape(frames, FT, width), zero_frame], 0)
    value_padded = jnp.concatenate([zero_frame, values.reshape(frames, FT, width), zero_frame], 0)
    key_blocks = keys.reshape(frames, blocks, BLOCK, width)
    value_blocks = values.reshape(frames, blocks, BLOCK, width)
    query_frames = queries.reshape(frames, FT, width)
    grad_frames = out_grad.reshape(frames, FT, width)
    slots = jnp.arange(frames, dtype=jnp.int32)

    def one_frame(carry, frame):
        near_acc, far_acc = carry
        pick_row = radial_pick[frame]
        chosen_block = (pick_row % blocks).astype(jnp.int32)
        near_k = lax.dynamic_slice_in_dim(key_padded, frame, 3, 0).reshape(3 * FT, width)
        near_v = lax.dynamic_slice_in_dim(value_padded, frame, 3, 0).reshape(3 * FT, width)
        far_k = key_blocks[slots, chosen_block].reshape(frames * BLOCK, width)
        far_v = value_blocks[slots, chosen_block].reshape(frames * BLOCK, width)
        key_h = jnp.concatenate([near_k, far_k], 0).reshape(-1, HEADS, HD).astype(jnp.float32)
        value_h = jnp.concatenate([near_v, far_v], 0).reshape(-1, HEADS, HD).astype(jnp.float32)
        live = frame_mask(frame, pick_row, frames)
        query_h = query_frames[frame].reshape(FT, HEADS, HD).astype(jnp.float32)
        grad_h = grad_frames[frame].reshape(FT, HEADS, HD).astype(jnp.float32)
        raw = jnp.einsum("qhd,khd->hqk", query_h, key_h) * scale
        masked = jnp.where(live[None], raw, -jnp.inf)
        top = jnp.max(masked, axis=2, keepdims=True)
        total = jnp.sum(jnp.exp(masked - top), axis=2, keepdims=True)
        lse = top + jnp.log(total)
        prob = jnp.exp(masked - lse)
        weights = lax.optimization_barrier(prob.astype(jnp.bfloat16))
        out_f = jnp.einsum("hqk,khd->qhd", weights.astype(jnp.float32), value_h)
        out_b = lax.optimization_barrier(out_f.astype(jnp.bfloat16))
        delta = jnp.einsum("qhd,qhd->hq", grad_h, out_b.astype(jnp.float32))[..., None]
        dprob = jnp.einsum("qhd,khd->hqk", grad_h, value_h)
        dscore = lax.optimization_barrier((prob * (dprob - delta)).astype(jnp.bfloat16)).astype(jnp.float32)
        query_grad = scale * jnp.einsum("hqk,khd->qhd", dscore, key_h)
        key_grad = (scale * jnp.einsum("hqk,qhd->khd", dscore, query_h)).reshape(-1, width)
        value_grad = jnp.einsum("hqk,qhd->khd", weights.astype(jnp.float32), grad_h).reshape(-1, width)
        near_part = jnp.stack([key_grad[:3 * FT], value_grad[:3 * FT]]).reshape(2, 3, FT, width)
        old = lax.dynamic_slice_in_dim(near_acc, frame, 3, 1)
        near_acc = lax.dynamic_update_slice_in_dim(near_acc, old + near_part, frame, 1)
        far_part = jnp.stack([key_grad[3 * FT:], value_grad[3 * FT:]]).reshape(2, frames, BLOCK, width)
        far_acc = far_acc.at[:, slots, chosen_block].add(far_part)
        outs = (out_b.reshape(FT, width), query_grad.reshape(FT, width).astype(jnp.bfloat16))
        return (near_acc, far_acc), outs

    near_init = jnp.zeros((2, frames + 2, FT, width), jnp.float32)
    far_init = jnp.zeros((2, frames, blocks, BLOCK, width), jnp.float32)
    (near_acc, far_acc), (attended, query_grad) = lax.scan(one_frame, (near_init, far_init), slots)
    grads = near_acc[:, 1:-1] + far_acc.reshape(2, frames, FT, width)
    key_grad = grads[0].reshape(TOKENS, width).astype(jnp.bfloat16)
    value_grad = grads[1].reshape(TOKENS, width).astype(jnp.bfloat16)
    return (attended.reshape(TOKENS, width), query_grad.reshape(TOKENS, width), key_grad, value_grad)
```

```python
import functools

import jax
import jax.numpy as jnp
from jax import lax
from jax.experimental import pallas as pl
from jax.experimental.pallas import tpu as pltpu
from jax.sharding import PartitionSpec as P

HD = 128
BLOCK = 64
NZ = 8
NY = 4
FT = 256
NEG = -1e30
FLOOR = -1e20
MESH = pl.DeviceIdType.MESH

NEAR, FAR0, FAR1, FAR2, FAR3, KEYS = 0, 256, 448, 576, 704, 768

NT = (((1,), (1,)), ((), ()))
NN = (((1,), (0,)), ((), ()))
TN = (((0,), (0,)), ((), ()))


def mm(a, b, dims):
    return lax.dot_general(a, b, dims, preferred_element_type=jnp.float32)


def kernel(
    pick_ref, q_ref, k_ref, v_ref, do_ref,
    out_ref, dq_ref, dk_ref, dv_ref,
    q_all, do_all, do_t, k_a, v_a, k_b, v_b, k_c, v_c, k_d, v_d,
    k_sel, v_sel, sc, st, fin, o_t, dq_t, o_send, o_recv, dq_send, dq_recv, acc, rs_send, rs_recv,
    z_ssem, z_rsem, y_ssem, y_rsem, r_ssem, r_rsem,
):
    width = q_ref.shape[1]
    heads = width // HD
    scale = HD ** -0.5
    me = lax.axis_index("ctx")
    z, y = me // NY, me % NY

    def at(dz, dy):
        return {"ctx": ((z + dz + NZ) % NZ) * NY + (y + dy) % NY}

    def cols(h):
        return slice(h * HD, (h + 1) * HD)

    barrier = pltpu.get_barrier_semaphore()
    for peer in (at(1, 0), at(-1, 0), at(0, 1), at(0, 2), at(0, 3)):
        pl.semaphore_signal(barrier, inc=1, device_id=peer, device_id_type=MESH)
    pl.semaphore_wait(barrier, 5)

    key_slot = {0: k_a.at[0], 1: k_a.at[1], -1: k_a.at[2], 2: k_b.at[0], -2: k_b.at[1],
                3: k_c.at[0], -3: k_c.at[1], 4: k_d.at[0], -4: k_d.at[0]}
    val_slot = {0: v_a.at[0], 1: v_a.at[1], -1: v_a.at[2], 2: v_b.at[0], -2: v_b.at[1],
                3: v_c.at[0], -3: v_c.at[1], 4: v_d.at[0], -4: v_d.at[0]}

    def z_copy(way, step, kind):
        sign = -1 if way == 0 else 1
        slots = (key_slot, val_slot)[kind]
        src = (k_ref, v_ref)[kind] if step == 1 else slots[sign * (step - 1)]
        return pltpu.make_async_remote_copy(
            src_ref=src,
            dst_ref=slots[sign * step],
            send_sem=z_ssem.at[way, step - 1, kind],
            recv_sem=z_rsem.at[way, step - 1, kind],
            device_id=at(-sign, 0),
            device_id_type=MESH,
        )

    def y_copy(src, dst, what, t):
        return pltpu.make_async_remote_copy(
            src_ref=src,
            dst_ref=dst,
            send_sem=y_ssem.at[what, t - 1],
            recv_sem=y_rsem.at[what, 3 - t],
            device_id=at(0, t),
            device_id_type=MESH,
        )

    sent = []

    def start(copy):
        copy.start()
        sent.append(copy)

    gather = {(w, s, k): z_copy(w, s, k) for w in (0, 1) for s in (1, 2, 3, 4) for k in (0, 1)}
    for kind in (0, 1):
        for way in (0, 1):
            start(gather[way, 1, kind])
    q_copies = [y_copy(q_ref, q_all.at[4 - t], 0, t) for t in (1, 3, 2)]
    do_copies = [y_copy(do_ref, do_all.at[4 - t], 1, t) for t in (1, 3, 2)]
    for copy in q_copies + do_copies:
        start(copy)

    k_a[0] = k_ref[...]
    v_a[0] = v_ref[...]
    q_all[0] = q_ref[...]
    do_all[0] = do_ref[...]

    @pl.loop(0, NY)
    def _(i):
        st[0, i, 0:heads] = jnp.full((heads, FT), FLOOR, jnp.float32)
        st[0, i, heads : 3 * heads] = jnp.zeros((2 * heads, FT), jnp.float32)
        o_t[i] = jnp.zeros((width, FT), jnp.float32)
        dq_t[i] = jnp.zeros((width, FT), jnp.float32)

    @pl.loop(0, NZ)
    def _(i):
        for kind in (0, 1):
            acc[i, kind] = jnp.zeros((FT, width), jnp.float32)

    tile = lax.broadcasted_iota(jnp.int32, (1, FT), 1) // BLOCK

    group0 = ((0, k_a, v_a, 0), (1, k_a, v_a, 1), (-1, k_a, v_a, 2))
    group1 = ((2, k_b, v_b, 0), (-2, k_b, v_b, 1))
    group2 = ((3, k_c, v_c, 0), (-3, k_c, v_c, 1))
    group3 = ((4, k_d, v_d, 0),)

    def chosen(qi, r):
        a = z * NY + (y + qi) % NY
        b = ((z + r + NZ) % NZ) * NY + y
        return pick_ref[a, b], jnp.abs(a - b)

    def bias_row(qi, r):
        pick, dist = chosen(qi, r)
        want = jnp.broadcast_to(pick, (1, FT)) >> 2
        row = jnp.where(tile == want, 0.0, NEG).astype(jnp.float32)
        row = jnp.maximum(row, jnp.where(dist < 4, 0.0, NEG).astype(jnp.float32))
        return jnp.minimum(row, jnp.where(dist < 2, NEG, 0.0).astype(jnp.float32))

    def select(group, begin):
        begin -= FAR0

        @pl.loop(0, NY)
        def _(qi):
            for g, (r, k, v, i) in enumerate(group):
                pick, _ = chosen(qi, r)
                place = jnp.broadcast_to(pick, (1, width)) & 3
                hits = [jnp.where(place == n, 1.0, 0.0).astype(k.dtype) for n in range(4)]
                to = slice(begin + g * BLOCK, begin + (g + 1) * BLOCK)
                for ref, dst in ((k, k_sel), (v, v_sel)):
                    parts = [ref[i, n * BLOCK : (n + 1) * BLOCK] * hits[n] for n in range(4)]
                    dst[qi, to] = (parts[0] + parts[1]) + (parts[2] + parts[3])

    def rows(parts):
        return parts[0] if len(parts) == 1 else jnp.concatenate(parts, 0)

    def update(qi, h, s, values):
        m_old = st[0, qi, h : h + 1]
        l_old = st[0, qi, heads + h : heads + h + 1]
        m_new = jnp.maximum(m_old, jnp.max(s, axis=0, keepdims=True))
        p = jnp.exp(s - m_new)
        alpha = jnp.exp(m_old - m_new)
        st[0, qi, h : h + 1] = m_new
        st[0, qi, heads + h : heads + h + 1] = l_old * alpha + jnp.sum(p, axis=0, keepdims=True)
        o_t[qi, cols(h)] = o_t[qi, cols(h)] * alpha + mm(values, p.astype(jnp.bfloat16), TN)

    def forward_far(group, begin):
        size = BLOCK * len(group)
        select(group, begin)

        @pl.loop(0, NY)
        def _(qi):
            bias = [bias_row(qi, r) for r, _, _, _ in group]
            bias = rows([jnp.broadcast_to(row, (BLOCK, FT)) for row in bias])
            for h in range(heads):
                ks = k_sel[qi, begin - FAR0 : begin - FAR0 + size, cols(h)]
                vs = v_sel[qi, begin - FAR0 : begin - FAR0 + size, cols(h)]
                s = mm(ks, q_all[qi, :, cols(h)], NT) * scale + bias
                sc[qi, h, begin : begin + size] = s
                update(qi, h, s, vs)

    def near_place(i):
        qi = jnp.where(i == 2, 3, i)
        over = ((i == 1) & (y == NY - 1)) | ((i == 2) & (y == 0))
        slot = jnp.where(over, jnp.where(i == 1, 2, 1), 0)
        r = jnp.where(over, jnp.where(i == 1, NZ - 1, 1), 0)
        dead = ((i == 1) & (y == NY - 1) & (z == 0)) | ((i == 2) & (y == 0) & (z == NZ - 1))
        return qi, slot, r, jnp.where(dead, NEG, 0.0).astype(jnp.float32)

    def forward_near():
        @pl.loop(0, 3)
        def _(i):
            qi, slot, _, bias = near_place(i)
            for h in range(heads):
                s = mm(k_a[slot, :, cols(h)], q_all[qi, :, cols(h)], NT) * scale + bias
                sc[qi, h, NEAR : NEAR + FT] = s
                update(qi, h, s, v_a[slot, :, cols(h)])

    def back(qi, h, begin, size, ks, vs):
        p = jnp.exp(sc[qi, h, begin : begin + size] - fin[qi, h : h + 1])
        grad = do_all[qi, :, cols(h)]
        dp = mm(vs, grad, NT)
        ds = (p * (dp - fin[qi, heads + h : heads + h + 1])).astype(jnp.bfloat16)
        dk = mm(ds, q_all[qi, :, cols(h)], NN) * scale
        dv = mm(p.astype(jnp.bfloat16), grad, NN)
        dq_t[qi, cols(h)] = dq_t[qi, cols(h)] + mm(ks, ds, TN)
        return dk, dv

    def backward_far(group, begin):
        size = BLOCK * len(group)

        @pl.loop(0, NY)
        def _(qi):
            for h in range(heads):
                ks = k_sel[qi, begin - FAR0 : begin - FAR0 + size, cols(h)]
                vs = v_sel[qi, begin - FAR0 : begin - FAR0 + size, cols(h)]
                parts = back(qi, h, begin, size, ks, vs)
                for g, (r, _, _, _) in enumerate(group):
                    pick, _ = chosen(qi, r)
                    place = jnp.broadcast_to(pick, (1, HD)) & 3
                    for n in range(FT // BLOCK):
                        hit = jnp.where(place == n, 1.0, 0.0).astype(jnp.float32)
                        where = slice(n * BLOCK, (n + 1) * BLOCK)
                        for kind in (0, 1):
                            part = parts[kind][g * BLOCK : (g + 1) * BLOCK]
                            acc[r % NZ, kind, where, cols(h)] += part * hit

    def backward_near():
        @pl.loop(0, 3)
        def _(i):
            qi, slot, r, _ = near_place(i)
            for h in range(heads):
                parts = back(qi, h, NEAR, FT, k_a[slot, :, cols(h)], v_a[slot, :, cols(h)])
                for kind in (0, 1):
                    acc[r, kind, :, cols(h)] += parts[kind]

    for kind in (0, 1):
        for way in (0, 1):
            gather[way, 1, kind].wait_recv()
            start(gather[way, 2, kind])
    for copy in q_copies:
        copy.wait_recv()
    forward_near()
    forward_far(group0, FAR0)
    for kind in (0, 1):
        for way in (0, 1):
            gather[way, 2, kind].wait_recv()
            start(gather[way, 3, kind])
    forward_far(group1, FAR1)
    for kind in (0, 1):
        for way in (0, 1):
            gather[way, 3, kind].wait_recv()
            if way == kind:
                start(gather[way, 4, kind])
    forward_far(group2, FAR2)
    for copy in do_copies:
        copy.wait_recv()

    @pl.loop(0, NY)
    def _(i):
        for h in range(heads):
            do_t[i, cols(h)] = do_all[i, :, cols(h)].astype(jnp.float32).T

    gather[0, 4, 0].wait_recv()
    gather[1, 4, 1].wait_recv()
    forward_far(group3, FAR3)

    @pl.loop(0, NY)
    def _(i):
        for h in range(heads):
            st[0, i, 2 * heads + h : 2 * heads + h + 1] = jnp.sum(
                o_t[i, cols(h)] * do_t[i, cols(h)], axis=0, keepdims=True
            )

    st_copies = [y_copy(st.at[0], st.at[4 - t], 2, t) for t in (2, 1, 3)]
    for copy in st_copies:
        start(copy)
    for copy in st_copies:
        copy.wait_recv()
    for qi in range(NY):
        peer = [st[s, (qi - s) % NY] for s in range(NY)]
        top = functools.reduce(jnp.maximum, [x[0:heads] for x in peer])
        gain = [jnp.exp(x[0:heads] - top) for x in peer]
        total = functools.reduce(jnp.add, [x[heads : 2 * heads] * g for x, g in zip(peer, gain)])
        delta = functools.reduce(
            jnp.add, [x[2 * heads : 3 * heads] * g for x, g in zip(peer, gain)]
        )
        fin[qi, 0:heads] = top + jnp.log(total)
        fin[qi, heads : 2 * heads] = delta / total
        fin[qi, 2 * heads : 3 * heads] = gain[0] / total

    def r_copy(way, step, kind):
        return pltpu.make_async_remote_copy(
            src_ref=rs_send.at[way, step, kind],
            dst_ref=rs_recv.at[way, step, kind],
            send_sem=r_ssem.at[way, step, kind],
            recv_sem=r_rsem.at[way, step, kind],
            device_id=at(1 if way == 0 else -1, 0),
            device_id_type=MESH,
        )

    scatter = {(w, s, k): r_copy(w, s, k) for w in (0, 1) for s in range(4) for k in (0, 1)}

    def pass_on(step, way, kind):
        r = (4 - step) if way == 0 else (step - 4) % NZ
        part = acc[r, kind]
        if step >= 2 or (step == 1 and way == kind):
            scatter[way, step - 1, kind].wait_recv()
            part = part + rs_recv[way, step - 1, kind].astype(jnp.float32)
        rs_send[way, step, kind] = part.astype(jnp.bfloat16)
        start(scatter[way, step, kind])

    backward_far(group3, FAR3)
    pass_on(0, 0, 0)
    pass_on(0, 1, 1)
    backward_far(group2, FAR2)
    for kind in (0, 1):
        for way in (0, 1):
            pass_on(1, way, 1 - kind if way == 0 else kind)

    o_copies = []
    for t in (2, 1, 3):
        for h in range(heads):
            weight = fin[t, 2 * heads + h : 2 * heads + h + 1]
            o_send[t - 1, cols(h)] = (o_t[t, cols(h)] * weight).astype(jnp.bfloat16)
        o_copies.append(y_copy(o_send.at[t - 1], o_recv.at[3 - t], 3, t))
        start(o_copies[-1])

    backward_far(group1, FAR1)
    for kind in (0, 1):
        for way in (0, 1):
            pass_on(2, way, kind)
    backward_near()
    backward_far(group0, FAR0)
    dq_copies = []
    for t in (2, 1, 3):
        dq_send[t - 1] = (dq_t[t] * scale).astype(jnp.bfloat16)
        dq_copies.append(y_copy(dq_send.at[t - 1], dq_recv.at[3 - t], 4, t))
        start(dq_copies[-1])
    for kind in (0, 1):
        for way in (0, 1):
            pass_on(3, way, kind)

    for copy in o_copies:
        copy.wait_recv()
    for h in range(heads):
        total = o_t[0, cols(h)] * fin[0, 2 * heads + h : 2 * heads + h + 1]
        for i in range(3):
            total = total + o_recv[i, cols(h)].astype(jnp.float32)
        out_ref[:, cols(h)] = total.T.astype(jnp.bfloat16)
    for copy in dq_copies:
        copy.wait_recv()
    for h in range(heads):
        total = dq_t[0, cols(h)] * scale
        for i in range(3):
            total = total + dq_recv[i, cols(h)].astype(jnp.float32)
        dq_ref[:, cols(h)] = total.T.astype(jnp.bfloat16)
    for kind, ref in ((0, dk_ref), (1, dv_ref)):
        total = acc[0, kind]
        for way in (0, 1):
            scatter[way, 3, kind].wait_recv()
            total = total + rs_recv[way, 3, kind].astype(jnp.float32)
        ref[...] = total.astype(jnp.bfloat16)
    for copy in sent:
        copy.wait_send()


def per_device(queries, keys, values, out_grad, radial_pick):
    width = queries.shape[1]
    heads = width // HD
    bf, f32 = jnp.bfloat16, jnp.float32
    vmem = pl.BlockSpec(memory_space=pltpu.VMEM)
    shape = jax.ShapeDtypeStruct((FT, width), bf)
    dma = pltpu.SemaphoreType.DMA
    return pl.pallas_call(
        kernel,
        out_shape=(shape,) * 4,
        in_specs=[pl.BlockSpec(memory_space=pltpu.SMEM)] + [vmem] * 4,
        out_specs=(vmem,) * 4,
        scratch_shapes=[
            pltpu.VMEM((NY, FT, width), bf),
            pltpu.VMEM((NY, FT, width), bf),
            pltpu.VMEM((NY, width, FT), f32),
            pltpu.VMEM((3, FT, width), bf),
            pltpu.VMEM((3, FT, width), bf),
            pltpu.VMEM((2, FT, width), bf),
            pltpu.VMEM((2, FT, width), bf),
            pltpu.VMEM((2, FT, width), bf),
            pltpu.VMEM((2, FT, width), bf),
            pltpu.VMEM((1, FT, width), bf),
            pltpu.VMEM((1, FT, width), bf),
            pltpu.VMEM((NY, KEYS - FAR0, width), bf),
            pltpu.VMEM((NY, KEYS - FAR0, width), bf),
            pltpu.VMEM((NY, heads, KEYS, FT), f32),
            pltpu.VMEM((NY, NY, 3 * heads, FT), f32),
            pltpu.VMEM((NY, 3 * heads, FT), f32),
            pltpu.VMEM((NY, width, FT), f32),
            pltpu.VMEM((NY, width, FT), f32),
            pltpu.VMEM((3, width, FT), bf),
            pltpu.VMEM((3, width, FT), bf),
            pltpu.VMEM((3, width, FT), bf),
            pltpu.VMEM((3, width, FT), bf),
            pltpu.VMEM((NZ, 2, FT, width), f32),
            pltpu.VMEM((2, 4, 2, FT, width), bf),
            pltpu.VMEM((2, 4, 2, FT, width), bf),
            dma((2, 4, 2)),
            dma((2, 4, 2)),
            dma((5, 3)),
            dma((5, 3)),
            dma((2, 4, 2)),
            dma((2, 4, 2)),
        ],
        compiler_params=pltpu.CompilerParams(
            collective_id=0, has_side_effects=True, vmem_limit_bytes=60 * 1024 * 1024
        ),
        name="radial_attention",
    )(radial_pick, queries, keys, values, out_grad)


def solution(mesh):
    spec = P(("dp", "ctx"), "head")
    return jax.shard_map(
        per_device,
        mesh=mesh,
        in_specs=(spec, spec, spec, spec, P()),
        out_specs=(spec,) * 4,
        check_vma=False,
    )
```

```python
import functools

import jax
import jax.numpy as jnp
from jax import lax
from jax.experimental import pallas as pl
from jax.experimental.pallas import tpu as pltpu
from jax.sharding import PartitionSpec as P

HD = 128
BLOCK = 64
NZ = 8
NY = 4
FT = 256
NEG = -1e30
FLOOR = -1e20
MESH = pl.DeviceIdType.MESH

NEAR, FAR0, FAR1, FAR2, FAR3, KEYS = 0, 256, 448, 576, 704, 768

NT = (((1,), (1,)), ((), ()))
NN = (((1,), (0,)), ((), ()))
TN = (((0,), (0,)), ((), ()))


def mm(a, b, dims):
    return lax.dot_general(a, b, dims, preferred_element_type=jnp.float32)


def kernel(
    pick_ref, q_ref, k_ref, v_ref, do_ref,
    out_ref, dq_ref, dk_ref, dv_ref,
    q_all, do_all, do_t, k_a, v_a, k_b, v_b, k_c, v_c, k_d, v_d,
    k_sel, v_sel, sc, st, fin, o_t, dq_t, o_send, o_recv, dq_send, dq_recv, acc, rs_send, rs_recv,
    z_ssem, z_rsem, y_ssem, y_rsem, r_ssem, r_rsem, l_sem,
):
    width = q_ref.shape[1]
    heads = width // HD
    scale = HD ** -0.5
    me = lax.axis_index("ctx")
    z, y = me // NY, me % NY

    def at(dz, dy):
        return {"ctx": ((z + dz + NZ) % NZ) * NY + (y + dy) % NY}

    def cols(h):
        return slice(h * HD, (h + 1) * HD)

    own = [
        pltpu.make_async_copy(src, dst.at[0], l_sem.at[i])
        for i, (src, dst) in enumerate(((k_ref, k_a), (v_ref, v_a), (q_ref, q_all), (do_ref, do_all)))
    ]
    for copy in own:
        copy.start()
    barrier = pltpu.get_barrier_semaphore()
    for peer in (at(1, 0), at(-1, 0), at(0, 1), at(0, 2), at(0, 3)):
        pl.semaphore_signal(barrier, inc=1, device_id=peer, device_id_type=MESH)
    pl.semaphore_wait(barrier, 5)

    key_slot = {0: k_a.at[0], 1: k_a.at[1], -1: k_a.at[2], 2: k_b.at[0], -2: k_b.at[1],
                3: k_c.at[0], -3: k_c.at[1], 4: k_d.at[0], -4: k_d.at[0]}
    val_slot = {0: v_a.at[0], 1: v_a.at[1], -1: v_a.at[2], 2: v_b.at[0], -2: v_b.at[1],
                3: v_c.at[0], -3: v_c.at[1], 4: v_d.at[0], -4: v_d.at[0]}

    def z_copy(way, step, kind):
        sign = -1 if way == 0 else 1
        slots = (key_slot, val_slot)[kind]
        src = (k_ref, v_ref)[kind] if step == 1 else slots[sign * (step - 1)]
        return pltpu.make_async_remote_copy(
            src_ref=src,
            dst_ref=slots[sign * step],
            send_sem=z_ssem.at[way, step - 1, kind],
            recv_sem=z_rsem.at[way, step - 1, kind],
            device_id=at(-sign, 0),
            device_id_type=MESH,
        )

    def y_copy(src, dst, what, t):
        return pltpu.make_async_remote_copy(
            src_ref=src,
            dst_ref=dst,
            send_sem=y_ssem.at[what, t - 1],
            recv_sem=y_rsem.at[what, 3 - t],
            device_id=at(0, t),
            device_id_type=MESH,
        )

    sent = []

    def start(copy):
        copy.start()
        sent.append(copy)

    gather = {
        (w, s, k): z_copy(w, s, k)
        for w in (0, 1) for s in (1, 2, 3, 4) for k in (0, 1) if s < 4 or w == k
    }
    for kind in (0, 1):
        for way in (0, 1):
            start(gather[way, 1, kind])
    q_copies = [y_copy(q_ref, q_all.at[4 - t], 0, t) for t in (1, 3, 2)]
    do_copies = [y_copy(do_ref, do_all.at[4 - t], 1, t) for t in (1, 3, 2)]
    for copy in q_copies + do_copies:
        start(copy)

    @pl.loop(0, NY)
    def _(i):
        st[0, i, 0:heads] = jnp.full((heads, FT), FLOOR, jnp.float32)
        st[0, i, heads : 3 * heads] = jnp.zeros((2 * heads, FT), jnp.float32)
        o_t[i] = jnp.zeros((width, FT), jnp.float32)
        dq_t[i] = jnp.zeros((width, FT), jnp.float32)

    @pl.loop(0, NZ)
    def _(i):
        for kind in (0, 1):
            acc[i, kind] = jnp.zeros((FT, width), jnp.float32)

    tile = lax.broadcasted_iota(jnp.int32, (1, FT), 1) // BLOCK

    group0 = ((0, k_a, v_a, 0), (1, k_a, v_a, 1), (-1, k_a, v_a, 2))
    group1 = ((2, k_b, v_b, 0), (-2, k_b, v_b, 1))
    group2 = ((3, k_c, v_c, 0), (-3, k_c, v_c, 1))
    group3 = ((4, k_d, v_d, 0),)

    def chosen(qi, r):
        a = z * NY + (y + qi) % NY
        b = ((z + r + NZ) % NZ) * NY + y
        return pick_ref[a, b], jnp.abs(a - b)

    def bias_row(qi, r):
        pick, dist = chosen(qi, r)
        want = jnp.broadcast_to(pick, (1, FT)) >> 2
        row = jnp.where(tile == want, 0.0, NEG).astype(jnp.float32)
        row = jnp.maximum(row, jnp.where(dist < 4, 0.0, NEG).astype(jnp.float32))
        return jnp.minimum(row, jnp.where(dist < 2, NEG, 0.0).astype(jnp.float32))

    def select(group, begin):
        begin -= FAR0

        @pl.loop(0, NY)
        def _(qi):
            for g, (r, k, v, i) in enumerate(group):
                pick, _ = chosen(qi, r)
                place = jnp.broadcast_to(pick, (1, width)) & 3
                hits = [jnp.where(place == n, 1.0, 0.0).astype(k.dtype) for n in range(4)]
                to = slice(begin + g * BLOCK, begin + (g + 1) * BLOCK)
                for ref, dst in ((k, k_sel), (v, v_sel)):
                    parts = [ref[i, n * BLOCK : (n + 1) * BLOCK] * hits[n] for n in range(4)]
                    dst[qi, to] = (parts[0] + parts[1]) + (parts[2] + parts[3])

    def rows(parts):
        return parts[0] if len(parts) == 1 else jnp.concatenate(parts, 0)

    def update(qi, h, s, values):
        m_old = st[0, qi, h : h + 1]
        l_old = st[0, qi, heads + h : heads + h + 1]
        m_new = jnp.maximum(m_old, jnp.max(s, axis=0, keepdims=True))
        p = jnp.exp(s - m_new)
        alpha = jnp.exp(m_old - m_new)
        st[0, qi, h : h + 1] = m_new
        st[0, qi, heads + h : heads + h + 1] = l_old * alpha + jnp.sum(p, axis=0, keepdims=True)
        o_t[qi, cols(h)] = o_t[qi, cols(h)] * alpha + mm(values, p.astype(jnp.bfloat16), TN)

    def forward_far(group, begin):
        size = BLOCK * len(group)
        select(group, begin)

        @pl.loop(0, NY)
        def _(qi):
            bias = [bias_row(qi, r) for r, _, _, _ in group]
            bias = rows([jnp.broadcast_to(row, (BLOCK, FT)) for row in bias])
            for h in range(heads):
                ks = k_sel[qi, begin - FAR0 : begin - FAR0 + size, cols(h)]
                vs = v_sel[qi, begin - FAR0 : begin - FAR0 + size, cols(h)]
                s = mm(ks, q_all[qi, :, cols(h)], NT) * scale + bias
                sc[qi, h, begin : begin + size] = s
                update(qi, h, s, vs)

    def near_place(i):
        qi = jnp.where(i == 2, 3, i)
        over = ((i == 1) & (y == NY - 1)) | ((i == 2) & (y == 0))
        slot = jnp.where(over, jnp.where(i == 1, 2, 1), 0)
        r = jnp.where(over, jnp.where(i == 1, NZ - 1, 1), 0)
        dead = ((i == 1) & (y == NY - 1) & (z == 0)) | ((i == 2) & (y == 0) & (z == NZ - 1))
        return qi, slot, r, jnp.where(dead, NEG, 0.0).astype(jnp.float32)

    def forward_near():
        @pl.loop(0, 3)
        def _(i):
            qi, slot, _, bias = near_place(i)
            for h in range(heads):
                s = mm(k_a[slot, :, cols(h)], q_all[qi, :, cols(h)], NT) * scale + bias
                sc[qi, h, NEAR : NEAR + FT] = s
                update(qi, h, s, v_a[slot, :, cols(h)])

    def back(qi, h, begin, size, ks, vs):
        p = jnp.exp(sc[qi, h, begin : begin + size] - fin[qi, h : h + 1])
        grad = do_all[qi, :, cols(h)]
        dp = mm(vs, grad, NT)
        ds = (p * (dp - fin[qi, heads + h : heads + h + 1])).astype(jnp.bfloat16)
        dk = mm(ds, q_all[qi, :, cols(h)], NN) * scale
        dv = mm(p.astype(jnp.bfloat16), grad, NN)
        dq_t[qi, cols(h)] = dq_t[qi, cols(h)] + mm(ks, ds, TN)
        return dk, dv

    def backward_far(group, begin):
        size = BLOCK * len(group)

        @pl.loop(0, NY)
        def _(qi):
            for h in range(heads):
                ks = k_sel[qi, begin - FAR0 : begin - FAR0 + size, cols(h)]
                vs = v_sel[qi, begin - FAR0 : begin - FAR0 + size, cols(h)]
                parts = back(qi, h, begin, size, ks, vs)
                for g, (r, _, _, _) in enumerate(group):
                    pick, _ = chosen(qi, r)
                    place = jnp.broadcast_to(pick, (1, HD)) & 3
                    for n in range(FT // BLOCK):
                        hit = jnp.where(place == n, 1.0, 0.0).astype(jnp.float32)
                        where = slice(n * BLOCK, (n + 1) * BLOCK)
                        for kind in (0, 1):
                            part = parts[kind][g * BLOCK : (g + 1) * BLOCK]
                            acc[r % NZ, kind, where, cols(h)] += part * hit

    def backward_near():
        @pl.loop(0, 3)
        def _(i):
            qi, slot, r, _ = near_place(i)
            for h in range(heads):
                parts = back(qi, h, NEAR, FT, k_a[slot, :, cols(h)], v_a[slot, :, cols(h)])
                for kind in (0, 1):
                    acc[r, kind, :, cols(h)] += parts[kind]

    for kind in (0, 1):
        for way in (0, 1):
            gather[way, 1, kind].wait_recv()
            start(gather[way, 2, kind])
    for copy in own:
        copy.wait()
    for copy in q_copies:
        copy.wait_recv()
    forward_near()
    forward_far(group0, FAR0)
    for kind in (0, 1):
        for way in (0, 1):
            gather[way, 2, kind].wait_recv()
            start(gather[way, 3, kind])
    forward_far(group1, FAR1)
    for kind in (0, 1):
        for way in (0, 1):
            gather[way, 3, kind].wait_recv()
            if way == kind:
                start(gather[way, 4, kind])
    forward_far(group2, FAR2)
    for copy in do_copies:
        copy.wait_recv()

    @pl.loop(0, NY)
    def _(i):
        for h in range(heads):
            do_t[i, cols(h)] = do_all[i, :, cols(h)].astype(jnp.float32).T

    gather[0, 4, 0].wait_recv()
    gather[1, 4, 1].wait_recv()
    forward_far(group3, FAR3)

    @pl.loop(0, NY)
    def _(i):
        for h in range(heads):
            st[0, i, 2 * heads + h : 2 * heads + h + 1] = jnp.sum(
                o_t[i, cols(h)] * do_t[i, cols(h)], axis=0, keepdims=True
            )

    st_copies = [y_copy(st.at[0], st.at[4 - t], 2, t) for t in (2, 1, 3)]
    for copy in st_copies:
        start(copy)
    for copy in st_copies:
        copy.wait_recv()
    for qi in range(NY):
        peer = [st[s, (qi - s) % NY] for s in range(NY)]
        top = functools.reduce(jnp.maximum, [x[0:heads] for x in peer])
        gain = [jnp.exp(x[0:heads] - top) for x in peer]
        total = functools.reduce(jnp.add, [x[heads : 2 * heads] * g for x, g in zip(peer, gain)])
        delta = functools.reduce(
            jnp.add, [x[2 * heads : 3 * heads] * g for x, g in zip(peer, gain)]
        )
        fin[qi, 0:heads] = top + jnp.log(total)
        fin[qi, heads : 2 * heads] = delta / total
        fin[qi, 2 * heads : 3 * heads] = gain[0] / total

    def r_copy(way, step, kind):
        return pltpu.make_async_remote_copy(
            src_ref=rs_send.at[way, step, kind],
            dst_ref=rs_recv.at[way, step, kind],
            send_sem=r_ssem.at[way, step, kind],
            recv_sem=r_rsem.at[way, step, kind],
            device_id=at(1 if way == 0 else -1, 0),
            device_id_type=MESH,
        )

    scatter = {
        (w, s, k): r_copy(w, s, k)
        for w in (0, 1) for s in range(4) for k in (0, 1) if s > 0 or w == k
    }

    def pass_on(step, way, kind):
        r = (4 - step) if way == 0 else (step - 4) % NZ
        part = acc[r, kind]
        if step >= 2 or (step == 1 and way == kind):
            scatter[way, step - 1, kind].wait_recv()
            part = part + rs_recv[way, step - 1, kind].astype(jnp.float32)
        rs_send[way, step, kind] = part.astype(jnp.bfloat16)
        start(scatter[way, step, kind])

    backward_far(group3, FAR3)
    pass_on(0, 0, 0)
    pass_on(0, 1, 1)
    backward_far(group2, FAR2)
    for kind in (0, 1):
        for way in (0, 1):
            pass_on(1, way, 1 - kind if way == 0 else kind)

    o_copies = []
    for t in (2, 1, 3):
        for h in range(heads):
            weight = fin[t, 2 * heads + h : 2 * heads + h + 1]
            o_send[t - 1, cols(h)] = (o_t[t, cols(h)] * weight).astype(jnp.bfloat16)
        o_copies.append(y_copy(o_send.at[t - 1], o_recv.at[3 - t], 3, t))
        start(o_copies[-1])

    backward_far(group1, FAR1)
    for kind in (0, 1):
        for way in (0, 1):
            pass_on(2, way, kind)
    backward_near()
    backward_far(group0, FAR0)
    dq_copies = []
    for t in (2, 1, 3):
        dq_send[t - 1] = (dq_t[t] * scale).astype(jnp.bfloat16)
        dq_copies.append(y_copy(dq_send.at[t - 1], dq_recv.at[3 - t], 4, t))
        start(dq_copies[-1])
    for kind in (0, 1):
        for way in (0, 1):
            pass_on(3, way, kind)

    for copy in o_copies:
        copy.wait_recv()
    for h in range(heads):
        total = o_t[0, cols(h)] * fin[0, 2 * heads + h : 2 * heads + h + 1]
        for i in range(3):
            total = total + o_recv[i, cols(h)].astype(jnp.float32)
        out_ref[:, cols(h)] = total.T.astype(jnp.bfloat16)
    for copy in dq_copies:
        copy.wait_recv()
    for h in range(heads):
        total = dq_t[0, cols(h)] * scale
        for i in range(3):
            total = total + dq_recv[i, cols(h)].astype(jnp.float32)
        dq_ref[:, cols(h)] = total.T.astype(jnp.bfloat16)
    for kind, ref in ((0, dk_ref), (1, dv_ref)):
        total = acc[0, kind]
        for way in (0, 1):
            scatter[way, 3, kind].wait_recv()
            total = total + rs_recv[way, 3, kind].astype(jnp.float32)
        ref[...] = total.astype(jnp.bfloat16)
    for copy in sent:
        copy.wait_send()


def hand_over(*refs):
    srcs, dsts, (buf, in_sem, out_sem) = refs[:4], refs[4:8], refs[8:]
    loads = [pltpu.make_async_copy(src, buf.at[i], in_sem.at[i]) for i, src in enumerate(srcs)]
    stores = [pltpu.make_async_copy(buf.at[i], dst, out_sem.at[i]) for i, dst in enumerate(dsts)]
    for load in loads:
        load.start()
    for load, store in zip(loads, stores):
        load.wait()
        store.start()
    for store in stores:
        store.wait()


def per_device(queries, keys, values, out_grad, radial_pick):
    width = queries.shape[1]
    heads = width // HD
    bf, f32 = jnp.bfloat16, jnp.float32
    vmem = pl.BlockSpec(memory_space=pltpu.VMEM)
    hbm = pl.BlockSpec(memory_space=pl.ANY)
    shape = jax.ShapeDtypeStruct((FT, width), bf)
    dma = pltpu.SemaphoreType.DMA
    outs = pl.pallas_call(
        kernel,
        out_shape=(shape,) * 4,
        in_specs=[pl.BlockSpec(memory_space=pltpu.SMEM)] + [hbm] * 4,
        out_specs=(vmem,) * 4,
        scratch_shapes=[
            pltpu.VMEM((NY, FT, width), bf),
            pltpu.VMEM((NY, FT, width), bf),
            pltpu.VMEM((NY, width, FT), f32),
            pltpu.VMEM((3, FT, width), bf),
            pltpu.VMEM((3, FT, width), bf),
            pltpu.VMEM((2, FT, width), bf),
            pltpu.VMEM((2, FT, width), bf),
            pltpu.VMEM((2, FT, width), bf),
            pltpu.VMEM((2, FT, width), bf),
            pltpu.VMEM((1, FT, width), bf),
            pltpu.VMEM((1, FT, width), bf),
            pltpu.VMEM((NY, KEYS - FAR0, width), bf),
            pltpu.VMEM((NY, KEYS - FAR0, width), bf),
            pltpu.VMEM((NY, heads, KEYS, FT), f32),
            pltpu.VMEM((NY, NY, 3 * heads, FT), f32),
            pltpu.VMEM((NY, 3 * heads, FT), f32),
            pltpu.VMEM((NY, width, FT), f32),
            pltpu.VMEM((NY, width, FT), f32),
            pltpu.VMEM((3, width, FT), bf),
            pltpu.VMEM((3, width, FT), bf),
            pltpu.VMEM((3, width, FT), bf),
            pltpu.VMEM((3, width, FT), bf),
            pltpu.VMEM((NZ, 2, FT, width), f32),
            pltpu.VMEM((2, 4, 2, FT, width), bf),
            pltpu.VMEM((2, 4, 2, FT, width), bf),
            dma((2, 4, 2)),
            dma((2, 4, 2)),
            dma((5, 3)),
            dma((5, 3)),
            dma((2, 4, 2)),
            dma((2, 4, 2)),
            dma((4,)),
        ],
        compiler_params=pltpu.CompilerParams(
            collective_id=0, has_side_effects=True, vmem_limit_bytes=60 * 1024 * 1024
        ),
        name="radial_attention",
    )(radial_pick, queries, keys, values, out_grad)
    return pl.pallas_call(
        hand_over,
        out_shape=(shape,) * 4,
        in_specs=[hbm] * 4,
        out_specs=(hbm,) * 4,
        scratch_shapes=[pltpu.VMEM((4, FT, width), bf), dma((4,)), dma((4,))],
        compiler_params=pltpu.CompilerParams(vmem_limit_bytes=60 * 1024 * 1024),
        name="hand_over",
    )(*outs)


def solution(mesh):
    spec = P(("dp", "ctx"), "head")
    return jax.shard_map(
        per_device,
        mesh=mesh,
        in_specs=(spec, spec, spec, spec, P()),
        out_specs=(spec,) * 4,
        check_vma=False,
    )
```

```python
import functools

import jax
import jax.numpy as jnp
from jax import lax
from jax.experimental import pallas as pl
from jax.experimental.pallas import tpu as pltpu
from jax.sharding import PartitionSpec as P

HD = 128
BLOCK = 64
NZ = 8
NY = 4
FT = 256
NEG = -1e30
FLOOR = -1e20
MESH = pl.DeviceIdType.MESH

NEAR, FAR0, FAR1, FAR2, FAR3, KEYS = 0, 256, 448, 576, 704, 768

NT = (((1,), (1,)), ((), ()))
NN = (((1,), (0,)), ((), ()))
TN = (((0,), (0,)), ((), ()))


def mm(a, b, dims):
    return lax.dot_general(a, b, dims, preferred_element_type=jnp.float32)


def kernel(
    pick_ref, q_ref, k_ref, v_ref, do_ref,
    out_ref, dq_ref, dk_ref, dv_ref,
    q_all, do_all, do_t, k_a, v_a, k_b, v_b, k_c, v_c, k_d, v_d,
    k_sel, v_sel, sc, run, st, dl, fin, o_t, dq_t, o_send, o_recv, dq_send, dq_recv, acc,
    rs_send, rs_recv,
    z_ssem, z_rsem, y_ssem, y_rsem, r_ssem, r_rsem, l_sem,
):
    width = q_ref.shape[1]
    heads = width // HD
    scale = HD ** -0.5
    half = FT // 2
    me = lax.axis_index("ctx")
    z, y = me // NY, me % NY

    def at(dz, dy):
        return {"ctx": ((z + dz + NZ) % NZ) * NY + (y + dy) % NY}

    def cols(h):
        return slice(h * HD, (h + 1) * HD)

    own = [
        pltpu.make_async_copy(src, dst.at[0], l_sem.at[i])
        for i, (src, dst) in enumerate(((k_ref, k_a), (v_ref, v_a), (q_ref, q_all), (do_ref, do_all)))
    ]
    for copy in own:
        copy.start()
    barrier = pltpu.get_barrier_semaphore()
    for peer in (at(1, 0), at(-1, 0), at(0, 1), at(0, 2), at(0, 3)):
        pl.semaphore_signal(barrier, inc=1, device_id=peer, device_id_type=MESH)
    pl.semaphore_wait(barrier, 5)

    places = {0: 0, 1: 1, -1: 2, 2: 0, -2: 1, 3: 0, -3: 1, 4: 0, -4: 0}
    stores = {0: (k_a, v_a), 1: (k_a, v_a), 2: (k_b, v_b), 3: (k_c, v_c), 4: (k_d, v_d)}

    def z_copy(way, step, kind, part):
        sign = -1 if way == 0 else 1
        rows = slice(0, FT) if part is None else slice(part * half, (part + 1) * half)
        if step == 1:
            src = (k_ref, v_ref)[kind].at[rows]
        else:
            src = stores[step - 1][kind].at[places[sign * (step - 1)], rows]
        return pltpu.make_async_remote_copy(
            src_ref=src,
            dst_ref=stores[step][kind].at[places[sign * step], rows],
            send_sem=z_ssem.at[way, step - 1, kind, part or 0],
            recv_sem=z_rsem.at[way, step - 1, kind, part or 0],
            device_id=at(-sign, 0),
            device_id_type=MESH,
        )

    def y_copy(src, dst, what, t):
        return pltpu.make_async_remote_copy(
            src_ref=src,
            dst_ref=dst,
            send_sem=y_ssem.at[what, t - 1],
            recv_sem=y_rsem.at[what, 3 - t],
            device_id=at(0, t),
            device_id_type=MESH,
        )

    sent = []

    def start(copy):
        copy.start()
        sent.append(copy)

    gather = {}

    def put(step, kind, part=None):
        for way in (0, 1):
            piece = None if part is None else way ^ part
            gather[way, step, kind, part] = z_copy(way, step, kind, piece)
            start(gather[way, step, kind, part])

    def got(step, kind, part=None):
        for way in (0, 1):
            gather[way, step, kind, part].wait_recv()

    put(1, 0)
    put(1, 1)
    q_copies = {t: y_copy(q_ref, q_all.at[4 - t], 0, t) for t in (1, 3, 2)}
    do_copies = {t: y_copy(do_ref, do_all.at[4 - t], 1, t) for t in (1, 3, 2)}
    for copy in list(q_copies.values()) + list(do_copies.values()):
        start(copy)

    @pl.loop(0, NY)
    def _(i):
        for j in (0, 1):
            run[j, i, 0:heads] = jnp.full((heads, FT), FLOOR, jnp.float32)
            run[j, i, heads : 2 * heads] = jnp.zeros((heads, FT), jnp.float32)
        o_t[i] = jnp.zeros((width, FT), jnp.float32)
        dq_t[i] = jnp.zeros((width, FT), jnp.float32)

    @pl.loop(0, NZ)
    def _(i):
        for kind in (0, 1):
            acc[i, kind] = jnp.zeros((FT, width), jnp.float32)

    tile = lax.broadcasted_iota(jnp.int32, (1, FT), 1) // BLOCK

    group0 = ((0, k_a, v_a, 0), (1, k_a, v_a, 1), (-1, k_a, v_a, 2))
    group1 = ((2, k_b, v_b, 0), (-2, k_b, v_b, 1))
    group2 = ((3, k_c, v_c, 0), (-3, k_c, v_c, 1))
    group3 = ((4, k_d, v_d, 0),)

    def chosen(qi, r):
        a = z * NY + (y + qi) % NY
        b = ((z + r + NZ) % NZ) * NY + y
        return pick_ref[a, b], jnp.abs(a - b)

    def bias_row(qi, r):
        pick, dist = chosen(qi, r)
        want = jnp.broadcast_to(pick, (1, FT)) >> 2
        row = jnp.where(tile == want, 0.0, NEG).astype(jnp.float32)
        row = jnp.maximum(row, jnp.where(dist < 4, 0.0, NEG).astype(jnp.float32))
        return jnp.minimum(row, jnp.where(dist < 2, NEG, 0.0).astype(jnp.float32))

    def select(group, begin, kinds):
        begin -= FAR0

        @pl.loop(0, NY)
        def _(qi):
            for g, (r, k, v, i) in enumerate(group):
                pick, _ = chosen(qi, r)
                place = jnp.broadcast_to(pick, (1, width)) & 3
                hits = [jnp.where(place == n, 1.0, 0.0).astype(k.dtype) for n in range(4)]
                to = slice(begin + g * BLOCK, begin + (g + 1) * BLOCK)
                for kind in kinds:
                    ref, dst = ((k, k_sel), (v, v_sel))[kind]
                    parts = [ref[i, n * BLOCK : (n + 1) * BLOCK] * hits[n] for n in range(4)]
                    dst[qi, to] = (parts[0] + parts[1]) + (parts[2] + parts[3])

    def rows(parts):
        return parts[0] if len(parts) == 1 else jnp.concatenate(parts, 0)

    def merge(j, qi, h, s):
        m_old = run[j, qi, h : h + 1]
        l_old = run[j, qi, heads + h : heads + h + 1]
        m_new = jnp.maximum(m_old, jnp.max(s, axis=0, keepdims=True))
        p = jnp.exp(s - m_new)
        alpha = jnp.exp(m_old - m_new)
        run[j, qi, h : h + 1] = m_new
        run[j, qi, heads + h : heads + h + 1] = l_old * alpha + jnp.sum(p, axis=0, keepdims=True)
        return p, alpha

    def update(qi, h, s, values):
        p, alpha = merge(0, qi, h, s)
        o_t[qi, cols(h)] = o_t[qi, cols(h)] * alpha + mm(values, p.astype(jnp.bfloat16), TN)

    def forward_far(group, begin, whole):
        size = BLOCK * len(group)
        select(group, begin, (0, 1) if whole else (0,))

        @pl.loop(0, NY)
        def _(qi):
            bias = [bias_row(qi, r) for r, _, _, _ in group]
            bias = rows([jnp.broadcast_to(row, (BLOCK, FT)) for row in bias])
            for h in range(heads):
                ks = k_sel[qi, begin - FAR0 : begin - FAR0 + size, cols(h)]
                s = mm(ks, q_all[qi, :, cols(h)], NT) * scale + bias
                sc[qi, h, begin : begin + size] = s
                if whole:
                    update(qi, h, s, v_sel[qi, begin - FAR0 : begin - FAR0 + size, cols(h)])
                else:
                    merge(1, qi, h, s)

    def near_place(i):
        qi = jnp.where(i == 2, 3, i)
        over = ((i == 1) & (y == NY - 1)) | ((i == 2) & (y == 0))
        slot = jnp.where(over, jnp.where(i == 1, 2, 1), 0)
        r = jnp.where(over, jnp.where(i == 1, NZ - 1, 1), 0)
        dead = ((i == 1) & (y == NY - 1) & (z == 0)) | ((i == 2) & (y == 0) & (z == NZ - 1))
        return qi, slot, r, jnp.where(dead, NEG, 0.0).astype(jnp.float32)

    def forward_near():
        @pl.loop(0, 3)
        def _(i):
            qi, slot, _, bias = near_place(i)
            for h in range(heads):
                s = mm(k_a[slot, :, cols(h)], q_all[qi, :, cols(h)], NT) * scale + bias
                sc[qi, h, NEAR : NEAR + FT] = s
                update(qi, h, s, v_a[slot, :, cols(h)])

    def scatter_add(group, qi, h, kind, value):
        for g, (r, _, _, _) in enumerate(group):
            pick, _ = chosen(qi, r)
            place = jnp.broadcast_to(pick, (1, HD)) & 3
            part = value[g * BLOCK : (g + 1) * BLOCK]
            for n in range(FT // BLOCK):
                hit = jnp.where(place == n, 1.0, 0.0).astype(jnp.float32)
                acc[r % NZ, kind, n * BLOCK : (n + 1) * BLOCK, cols(h)] += part * hit

    def value_part(qi, h, p):
        return mm(p.astype(jnp.bfloat16), do_all[qi, :, cols(h)], NN)

    def key_part(qi, h, p, ks, vs):
        dp = mm(vs, do_all[qi, :, cols(h)], NT)
        ds = (p * (dp - fin[qi, heads + h : heads + h + 1])).astype(jnp.bfloat16)
        dq_t[qi, cols(h)] = dq_t[qi, cols(h)] + mm(ks, ds, TN)
        return mm(ds, q_all[qi, :, cols(h)], NN) * scale

    def backward_far(group, begin, kinds):
        size = BLOCK * len(group)

        @pl.loop(0, NY)
        def _(qi):
            for h in range(heads):
                p = sc[qi, h, begin : begin + size]
                if 1 in kinds:
                    p = jnp.exp(p - fin[qi, h : h + 1])
                    if 0 not in kinds:
                        sc[qi, h, begin : begin + size] = p
                    scatter_add(group, qi, h, 1, value_part(qi, h, p))
                if 0 in kinds:
                    ks = k_sel[qi, begin - FAR0 : begin - FAR0 + size, cols(h)]
                    vs = v_sel[qi, begin - FAR0 : begin - FAR0 + size, cols(h)]
                    scatter_add(group, qi, h, 0, key_part(qi, h, p, ks, vs))

    def backward_near():
        @pl.loop(0, 3)
        def _(i):
            qi, slot, r, _ = near_place(i)
            for h in range(heads):
                p = jnp.exp(sc[qi, h, NEAR : NEAR + FT] - fin[qi, h : h + 1])
                acc[r, 1, :, cols(h)] += value_part(qi, h, p)
                ks, vs = k_a[slot, :, cols(h)], v_a[slot, :, cols(h)]
                acc[r, 0, :, cols(h)] += key_part(qi, h, p, ks, vs)

    got(1, 0)
    put(2, 0)
    got(1, 1)
    put(2, 1, 0)
    for copy in own:
        copy.wait()
    q_copies[1].wait_recv()
    q_copies[3].wait_recv()
    forward_near()
    got(2, 0)
    put(3, 0)
    put(2, 1, 1)
    q_copies[2].wait_recv()
    forward_far(group0, FAR0, True)
    got(3, 0)
    put(4, 0, 0)
    got(2, 1, 0)
    put(3, 1, 0)
    forward_far(group2, FAR2, False)
    got(2, 1, 1)
    put(3, 1, 1)
    forward_far(group1, FAR1, True)
    got(4, 0, 0)
    forward_far(group3, FAR3, False)

    for qi in range(NY):
        m = [run[j, qi, 0:heads] for j in (0, 1)]
        l = [run[j, qi, heads : 2 * heads] for j in (0, 1)]
        top = jnp.maximum(m[0], m[1])
        st[0, qi, 0:heads] = top
        st[0, qi, heads : 2 * heads] = l[0] * jnp.exp(m[0] - top) + l[1] * jnp.exp(m[1] - top)
    st_copies = [y_copy(st.at[0], st.at[4 - t], 2, t) for t in (2, 1, 3)]
    for copy in st_copies:
        start(copy)
    got(3, 1, 0)
    put(4, 1, 0)
    for copy in do_copies.values():
        copy.wait_recv()

    @pl.loop(0, NY)
    def _(i):
        for h in range(heads):
            do_t[i, cols(h)] = do_all[i, :, cols(h)].astype(jnp.float32).T

    for copy in st_copies:
        copy.wait_recv()
    for qi in range(NY):
        peer = [st[s, (qi - s) % NY] for s in range(NY)]
        top = functools.reduce(jnp.maximum, [x[0:heads] for x in peer])
        total = functools.reduce(
            jnp.add, [x[heads : 2 * heads] * jnp.exp(x[0:heads] - top) for x in peer]
        )
        fin[qi, 0:heads] = top + jnp.log(total)

    scatter = {}

    def pass_on(step, kind, part):
        for way in (0, 1):
            r = (4 - step) if way == 0 else (step - 4) % NZ
            piece = way ^ part
            where = slice(piece * half, (piece + 1) * half)
            value = acc[r, kind, where]
            if step >= 2 or (step == 1 and part == 0):
                scatter[way, step - 1, kind, part].wait_recv()
                value = value + rs_recv[way, step - 1, kind, where].astype(jnp.float32)
            rs_send[way, step, kind, where] = value.astype(jnp.bfloat16)
            copy = pltpu.make_async_remote_copy(
                src_ref=rs_send.at[way, step, kind, where],
                dst_ref=rs_recv.at[way, step, kind, where],
                send_sem=r_ssem.at[way, step, kind, part],
                recv_sem=r_rsem.at[way, step, kind, part],
                device_id=at(1 if way == 0 else -1, 0),
                device_id_type=MESH,
            )
            scatter[way, step, kind, part] = copy
            start(copy)

    backward_far(group3, FAR3, (1,))
    pass_on(0, 1, 0)
    backward_far(group2, FAR2, (1,))
    pass_on(1, 1, 1)
    got(3, 1, 1)
    got(4, 1, 0)
    select(group2, FAR2, (1,))
    select(group3, FAR3, (1,))

    @pl.loop(0, NY)
    def _(qi):
        for h in range(heads):
            p = sc[qi, h, FAR2:KEYS].astype(jnp.bfloat16)
            vs = v_sel[qi, FAR2 - FAR0 : KEYS - FAR0, cols(h)]
            keep = jnp.exp(run[0, qi, h : h + 1] - fin[qi, h : h + 1])
            o = o_t[qi, cols(h)] * keep + mm(vs, p, TN)
            o_t[qi, cols(h)] = o
            dl[0, qi, h : h + 1] = jnp.sum(o * do_t[qi, cols(h)], axis=0, keepdims=True)

    dl_copies = [y_copy(dl.at[0], dl.at[4 - t], 5, t) for t in (2, 1, 3)]
    for copy in dl_copies:
        start(copy)
    pass_on(1, 1, 0)
    o_copies = []
    for t in (2, 1, 3):
        o_send[t - 1] = o_t[t].astype(jnp.bfloat16)
        o_copies.append(y_copy(o_send.at[t - 1], o_recv.at[3 - t], 3, t))
        start(o_copies[-1])
    backward_far(group1, FAR1, (1,))
    pass_on(2, 1, 1)
    for copy in dl_copies:
        copy.wait_recv()
    for qi in range(NY):
        fin[qi, heads : 2 * heads] = functools.reduce(
            jnp.add, [dl[s, (qi - s) % NY] for s in range(NY)]
        )
    pass_on(2, 1, 0)
    backward_far(group3, FAR3, (0,))
    pass_on(0, 0, 0)
    backward_far(group2, FAR2, (0,))
    pass_on(1, 0, 1)
    backward_far(group1, FAR1, (0,))
    pass_on(1, 0, 0)
    backward_far(group0, FAR0, (0, 1))
    dq_copies = []

    def send_dq(t):
        dq_send[t - 1] = (dq_t[t] * scale).astype(jnp.bfloat16)
        dq_copies.append(y_copy(dq_send.at[t - 1], dq_recv.at[3 - t], 4, t))
        start(dq_copies[-1])

    send_dq(2)
    pass_on(2, 0, 1)
    backward_near()
    send_dq(1)
    send_dq(3)
    pass_on(3, 1, 1)
    pass_on(2, 0, 0)
    pass_on(3, 1, 0)
    pass_on(3, 0, 1)
    pass_on(3, 0, 0)

    for copy in o_copies:
        copy.wait_recv()
    for h in range(heads):
        total = o_t[0, cols(h)]
        for i in range(3):
            total = total + o_recv[i, cols(h)].astype(jnp.float32)
        out_ref[:, cols(h)] = total.T.astype(jnp.bfloat16)
    for copy in dq_copies:
        copy.wait_recv()
    for h in range(heads):
        total = dq_t[0, cols(h)] * scale
        for i in range(3):
            total = total + dq_recv[i, cols(h)].astype(jnp.float32)
        dq_ref[:, cols(h)] = total.T.astype(jnp.bfloat16)
    for kind, ref in ((1, dv_ref), (0, dk_ref)):
        for way in (0, 1):
            for part in (0, 1):
                scatter[way, 3, kind, part].wait_recv()
        total = acc[0, kind]
        for way in (0, 1):
            total = total + rs_recv[way, 3, kind].astype(jnp.float32)
        ref[...] = total.astype(jnp.bfloat16)
    for copy in sent:
        copy.wait_send()


def hand_over(*refs):
    srcs, dsts, (buf, in_sem, out_sem) = refs[:4], refs[4:8], refs[8:]
    loads = [pltpu.make_async_copy(src, buf.at[i], in_sem.at[i]) for i, src in enumerate(srcs)]
    stores = [pltpu.make_async_copy(buf.at[i], dst, out_sem.at[i]) for i, dst in enumerate(dsts)]
    for load in loads:
        load.start()
    for load, store in zip(loads, stores):
        load.wait()
        store.start()
    for store in stores:
        store.wait()


def per_device(queries, keys, values, out_grad, radial_pick):
    width = queries.shape[1]
    heads = width // HD
    bf, f32 = jnp.bfloat16, jnp.float32
    vmem = pl.BlockSpec(memory_space=pltpu.VMEM)
    hbm = pl.BlockSpec(memory_space=pl.ANY)
    shape = jax.ShapeDtypeStruct((FT, width), bf)
    dma = pltpu.SemaphoreType.DMA
    outs = pl.pallas_call(
        kernel,
        out_shape=(shape,) * 4,
        in_specs=[pl.BlockSpec(memory_space=pltpu.SMEM)] + [hbm] * 4,
        out_specs=(vmem,) * 4,
        scratch_shapes=[
            pltpu.VMEM((NY, FT, width), bf),
            pltpu.VMEM((NY, FT, width), bf),
            pltpu.VMEM((NY, width, FT), f32),
            pltpu.VMEM((3, FT, width), bf),
            pltpu.VMEM((3, FT, width), bf),
            pltpu.VMEM((2, FT, width), bf),
            pltpu.VMEM((2, FT, width), bf),
            pltpu.VMEM((2, FT, width), bf),
            pltpu.VMEM((2, FT, width), bf),
            pltpu.VMEM((1, FT, width), bf),
            pltpu.VMEM((1, FT, width), bf),
            pltpu.VMEM((NY, KEYS - FAR0, width), bf),
            pltpu.VMEM((NY, KEYS - FAR0, width), bf),
            pltpu.VMEM((NY, heads, KEYS, FT), f32),
            pltpu.VMEM((2, NY, 2 * heads, FT), f32),
            pltpu.VMEM((NY, NY, 2 * heads, FT), f32),
            pltpu.VMEM((NY, NY, heads, FT), f32),
            pltpu.VMEM((NY, 2 * heads, FT), f32),
            pltpu.VMEM((NY, width, FT), f32),
            pltpu.VMEM((NY, width, FT), f32),
            pltpu.VMEM((3, width, FT), bf),
            pltpu.VMEM((3, width, FT), bf),
            pltpu.VMEM((3, width, FT), bf),
            pltpu.VMEM((3, width, FT), bf),
            pltpu.VMEM((NZ, 2, FT, width), f32),
            pltpu.VMEM((2, 4, 2, FT, width), bf),
            pltpu.VMEM((2, 4, 2, FT, width), bf),
            dma((2, 4, 2, 2)),
            dma((2, 4, 2, 2)),
            dma((6, 3)),
            dma((6, 3)),
            dma((2, 4, 2, 2)),
            dma((2, 4, 2, 2)),
            dma((4,)),
        ],
        compiler_params=pltpu.CompilerParams(
            collective_id=0, has_side_effects=True, vmem_limit_bytes=60 * 1024 * 1024
        ),
        name="radial_attention",
    )(radial_pick, queries, keys, values, out_grad)
    return pl.pallas_call(
        hand_over,
        out_shape=(shape,) * 4,
        in_specs=[hbm] * 4,
        out_specs=(hbm,) * 4,
        scratch_shapes=[pltpu.VMEM((4, FT, width), bf), dma((4,)), dma((4,))],
        compiler_params=pltpu.CompilerParams(vmem_limit_bytes=60 * 1024 * 1024),
        name="hand_over",
    )(*outs)


def solution(mesh):
    spec = P(("dp", "ctx"), "head")
    return jax.shard_map(
        per_device,
        mesh=mesh,
        in_specs=(spec, spec, spec, spec, P()),
        out_specs=(spec,) * 4,
        check_vma=False,
    )
```
